32 devices in a mesh: groups: 2 (over x), row: 16 (over z, y, core).
Axes of the slice: x: 2, y: 2, z: 4, core: 2. Of those that a mesh axis runs over, the one named last changes fastest.
Arguments:
- orbitals: bfloat16 [4096, 512], P(('groups', 'row')), parts along dimension 0, may hold values from -1.296875 to 1.296875
- basis: bfloat16 [4096, 1024], P(('groups', 'row')), parts along dimension 0, may hold values from -0.1875 to 0.1875
- kernel: bfloat16 [4096, 2048], P(('groups', 'row')), parts along dimension 0, may hold values from -6 to 6
Outputs:
- exchange_matrix: float32 [2048, 1024], P('groups', 'row'), parts along dimension 0
The draws below stay inside these ranges and needn't reach their ends.
There are 2 independent parts, one for each index of `groups`. The reference program is written for one: setup_inputs(seed, part) draws one part's arguments, and reference() takes and returns one part's arrays. A program takes and returns all parts, laid end to end along the dimension named above; each array names one. Nothing has to cross between parts.
All inputs are finite; a program needn't handle non-finite values.
Results may differ from the reference program's by a relative error of at most 0.0041.
Values may be sent and summed in bfloat16 or wider, within the bound.
A program may use at most 128 MiB of HBM per device.

```python
import jax
import jax.numpy as jnp
from jax import lax

NOCC = 512
NB = 1024
NP = 2048


def spiked(entries, stream_key, source, target, parts, factor):
    owner, partner = [(jnp.arange(entries.shape[axis_at]) // (entries.shape[axis_at] // parts)).reshape([-1 if axis == axis_at else 1 for axis in range(entries.ndim)]) for axis_at in (source, target)]
    chosen = jax.random.permutation(stream_key, parts)[partner]
    strong = (owner == chosen) | (owner == (partner + parts // 2) % parts)
    return jnp.where(strong, factor * entries, entries)


def steps_of(own_key, shape, split, smallest, high):
    def one(dim, parts):
        draws = jax.random.uniform(jax.random.fold_in(jax.random.fold_in(own_key, 6), dim), (parts,), jnp.float32, smallest / len(split), high / len(split))
        return jnp.repeat(jnp.exp(draws), shape[dim] // parts).reshape((-1,) + (1,) * (len(shape) - dim - 1))

    loudness = one(*split[0])
    for cut in split[1:]:
        loudness = loudness * one(*cut)
    return loudness


def noise(stream_key, shape, spread, most, shards=(), kind=jnp.bfloat16):
    drawn = spread * jax.random.normal(stream_key, shape, jnp.float32)
    if shards:
        drawn = drawn * steps_of(stream_key, shape, shards, -0.22, 0.18)
    return jnp.clip(drawn, -most, most).astype(kind)


def noise_with(stream_key, extent, scale, reach, cuts, heavy, held_as=jnp.bfloat16):
    result = scale * jax.random.normal(stream_key, extent, jnp.float32)
    if cuts:
        result = result * steps_of(stream_key, extent, cuts, -0.22, 0.18)
    return jnp.clip(spiked(result, jax.random.fold_in(stream_key, 3), *heavy), -reach, reach).astype(held_as)


def setup_inputs(seed: int = 0, part: int = 0) -> dict:
    streams_of = jax.random.split(jax.random.key(seed), 4)
    part_splits = jax.random.split(jax.random.fold_in(streams_of[3], part), 4)
    return {
        "orbitals": noise(part_splits[0], (NP, NOCC), 0.21, 1.296875, ((0, 16),)),
        "basis": noise_with(part_splits[1], (NP, NB), NP ** -0.5, 0.1875, ((0, 16),), (0, 1, 16, 2.0)),
        "kernel": noise(part_splits[2], (NP, NP), 1.0, 6.0, ((0, 16),)),
    }


def reference(orbitals, basis, kernel):
    density = lax.dot_general(orbitals, orbitals, (((1,), (1,)), ((), ())), preferred_element_type=jnp.float32)
    weighted = (density * kernel.astype(jnp.float32)).astype(jnp.bfloat16)
    applied = jnp.dot(weighted, basis, preferred_element_type=jnp.float32).astype(jnp.bfloat16)
    return lax.dot_general(basis, applied, (((0,), (0,)), ((), ())), preferred_element_type=jnp.float32)
```

```python
import functools

import jax
import jax.numpy as jnp
from jax import lax
from jax.experimental import pallas as pl
from jax.experimental.pallas import tpu as pltpu
from jax.sharding import PartitionSpec as P

LANES = 128
MESH = pl.DeviceIdType.MESH


def layout(mesh):
    n = mesh.shape["row"]
    try:
        line = mesh.devices[0]
        places = [tuple(d.coords) + (d.core_on_chip,) for d in line]
    except AttributeError:
        return n, 1, 1
    cores = len({p[-1] for p in places})
    axes = [a for a in range(3) if len({p[a] for p in places}) > 1]
    sizes = {a: len({p[a] for p in places}) for a in axes}
    for axis_z in axes:
        rest = [a for a in axes if a != axis_z]
        if len(rest) > 1 or (rest and sizes[rest[0]] != 2):
            continue
        y_size = sizes[rest[0]] if rest else 1
        z0 = min(p[axis_z] for p in places)
        y0 = min(p[rest[0]] for p in places) if rest else 0
        found = [
            ((p[axis_z] - z0) * y_size + (p[rest[0]] - y0 if rest else 0)) * cores + p[-1]
            for p in places
        ]
        if found == list(range(n)):
            return sizes[axis_z], y_size, cores
    return n, 1, 1


def kernel(
    dims, o_in, b_in, k_in, out_ref,
    o_all, b_all, k_v, w, app_t, got, in_sem, send_sem, recv_sem, a2a_send, a2a_recv,
):
    Z, Y, C = dims
    n = Z * Y * C
    units = Z * Y
    parts = 3
    rows = o_in.shape[0]
    half_cols = b_all.shape[-1]
    groups = half_cols // LANES
    cw = app_t.shape[0] * app_t.shape[1] // n
    per = LANES // cw

    me = lax.axis_index("row")
    c = me % C
    y = (me // C) % Y
    z = me // (C * Y)
    peer_y = (Y - 1) - y

    def index(zz, yy, cc):
        return (zz * Y + yy) * C + cc

    up_dev = index(jnp.minimum(z + 1, Z - 1), y, c)
    down_dev = index(jnp.maximum(z - 1, 0), y, c)
    y_dev = index(z, peer_y, c)
    sib_dev = index(z, y, (C - 1) - c)
    has_up = z < Z - 1
    has_down = z > 0

    def chunk(i, p):
        return o_all.at[i] if p == 0 else b_all.at[p - 1, i]

    def copy(i, p, kind):
        dev = (up_dev, down_dev, y_dev, sib_dev)[kind]
        return pltpu.make_async_remote_copy(
            src_ref=chunk(i, p),
            dst_ref=chunk(i, p),
            send_sem=send_sem.at[kind, p, i // C],
            recv_sem=recv_sem.at[p, i],
            device_id={"row": dev},
            device_id_type=MESH,
        )

    def wait_recv(i, p):
        copy(i, p, 3).wait_recv()

    loads = [pltpu.make_async_copy(o_in, o_all.at[me], in_sem.at[0])]
    for g in range(2 * groups):
        h, s = g % 2, g // 2
        loads.append(
            pltpu.make_async_copy(
                b_in.at[:, pl.ds(g * LANES, LANES)],
                b_all.at[h, me, :, pl.ds(s * LANES, LANES)],
                in_sem.at[1 + g],
            )
        )
    k_load = pltpu.make_async_copy(k_in, k_v, in_sem.at[1 + 2 * groups])
    for load in loads:
        load.start()
    k_load.start()

    barrier = pltpu.get_barrier_semaphore()

    def greet(dev):
        pl.semaphore_signal(barrier, inc=1, device_id={"row": dev}, device_id_type=MESH)

    pl.when(has_up)(lambda: greet(up_dev))
    pl.when(has_down)(lambda: greet(down_dev))
    if Y > 1:
        greet(y_dev)
    if C > 1:
        greet(sib_dev)
    others = (Y > 1) + (C > 1)
    pl.semaphore_wait(barrier, others + has_up.astype(jnp.int32) + has_down.astype(jnp.int32))

    def spread(i, p, up=False, down=False, across=False):
        if up:
            pl.when(has_up)(lambda: copy(i, p, 0).start())
        if down:
            pl.when(has_down)(lambda: copy(i, p, 1).start())
        if across and Y > 1:
            copy(i, p, 2).start()
        if C > 1:
            copy(i, p, 3).start()

    def own(p):
        if p == 0:
            loads[0].wait()
        else:
            for g in range(2 * groups):
                if g % 2 == p - 1:
                    loads[1 + g].wait()
        spread(me, p, up=True, down=True, across=True)

    def along(p, t):
        def low():
            i = index(z - t, y, c)
            wait_recv(i, p)
            spread(i, p, up=True, across=True)

        def high():
            i = index(z + t, y, c)
            wait_recv(i, p)
            spread(i, p, down=True, across=True)

        pl.when(z - t >= 0)(low)
        pl.when(z + t < Z)(high)

    def across(p, t):
        def one(zz):
            i = index(zz, peer_y, c)
            wait_recv(i, p)
            spread(i, p)

        if t == 0:
            one(z)
        else:
            pl.when(z - t >= 0)(lambda: one(z - t))
            pl.when(z + t < Z)(lambda: one(z + t))

    events = []
    for p in range(parts):
        events.append((p * (Z - 1) + 0.5 * (p > 0), p, functools.partial(own, p)))
        for t in range(1, Z):
            events.append((p * (Z - 1) + t, p, functools.partial(along, p, t)))
        if Y > 1:
            for t in range(Z):
                events.append((p * Z + t + 1 + 0.6 * (t > 0), p, functools.partial(across, p, t)))
    events.sort(key=lambda e: e[0])
    last = [max(k for k, e in enumerate(events) if e[1] == p) for p in range(parts)]

    def wait_sibling(p, u):
        if C > 1:
            wait_recv(u * C + (C - 1) - c, p)

    def weigh(u):
        if u == 0:
            k_load.wait()
        wait_sibling(0, u)
        cols = pl.ds(u * C * rows, C * rows)
        block = o_all[u * C:(u + 1) * C].reshape(C * rows, o_all.shape[-1])
        density = lax.dot_general(
            o_all[me], block, (((1,), (1,)), ((), ())), preferred_element_type=jnp.float32
        )
        w[:, cols] = (density * k_v[:, cols].astype(jnp.float32)).astype(jnp.bfloat16)

    wide = 2 * LANES if groups % 2 == 0 else LANES
    depth = min(n, max(1, 2048 // rows))

    def apply(h, j):
        if j == 0:
            for u in range(units):
                wait_sibling(1 + h, u)
        cols = pl.ds(j * wide, wide)

        def term(q):
            block = b_all[h, pl.ds(q * depth, depth), :, cols].reshape(depth * rows, wide)
            return jnp.dot(
                w[:, pl.ds(pl.multiple_of(q * depth * rows, LANES), depth * rows)],
                block,
                preferred_element_type=jnp.float32,
            )

        if n == depth:
            total = term(0)
        else:
            total = lax.fori_loop(
                0, n // depth, lambda q, a: a + term(q), jnp.zeros((rows, wide), jnp.float32)
            )
        app_t[h, cols, :] = total.astype(jnp.bfloat16).T

    count = n // 2

    def exchange(h, q):
        qq = (q + me) % count
        s, e = qq // per, qq % per
        d = (2 * s + h) * per + e
        off = pl.multiple_of(s * LANES + e * cw, 16)
        return d, pltpu.make_async_remote_copy(
            src_ref=app_t.at[h, pl.ds(off, cw), :],
            dst_ref=got.at[:, pl.ds(pl.multiple_of(me * rows, LANES), rows)],
            send_sem=a2a_send.at[h, q],
            recv_sem=a2a_recv.at[me],
            device_id={"row": d},
            device_id_type=MESH,
        ), pltpu.make_async_copy(
            app_t.at[h, pl.ds(off, cw), :],
            got.at[:, pl.ds(pl.multiple_of(me * rows, LANES), rows)],
            a2a_recv.at[me],
        )

    def hand_out(h):
        for q in range(count):
            d, remote, local = exchange(h, q)
            pl.when(d != me)(lambda: remote.start())
            pl.when(d == me)(lambda: local.start())

    work = {p: [] for p in range(parts)}
    for u in range(units):
        work[0].append(functools.partial(weigh, u))
    for h in range(2):
        for j in range(half_cols // wide):
            work[1 + h].append(functools.partial(apply, h, j))
        work[1 + h].append(functools.partial(hand_out, h))

    queue = []
    for k, (_, _, event) in enumerate(events):
        event()
        if queue:
            queue.pop(0)()
        for p in range(parts):
            if last[p] == k:
                queue.extend(work[p])
    for item in queue:
        item()

    for src in range(n):
        pltpu.make_async_copy(
            got.at[:, pl.ds(src * rows, rows)], got.at[:, pl.ds(src * rows, rows)], a2a_recv.at[src]
        ).wait()
    for h in range(2):
        for j in range(half_cols // wide):
            cols = pl.ds(j * wide, wide)

            def term(q):
                block = b_all[h, pl.ds(q * depth, depth), :, cols].reshape(depth * rows, wide)
                return jnp.dot(
                    got[:, pl.ds(pl.multiple_of(q * depth * rows, LANES), depth * rows)],
                    block,
                    preferred_element_type=jnp.float32,
                )

            if n == depth:
                total = term(0)
            else:
                total = lax.fori_loop(
                    0, n // depth, lambda q, a: a + term(q), jnp.zeros((cw, wide), jnp.float32)
                )
            for v in range(wide // LANES):
                g = 2 * (j * (wide // LANES) + v) + h
                out_ref[pl.ds(g * LANES, LANES), :] = total[:, v * LANES:(v + 1) * LANES].T

    for h in range(2):
        for q in range(count):
            d, remote, _ = exchange(h, q)
            pl.when(d != me)(lambda: remote.wait_send())
    for p in range(parts):
        for zz in range(Z):
            i = index(zz, y, c)
            pl.when(jnp.logical_and(has_up, zz <= z))(lambda: copy(i, p, 0).wait_send())
            pl.when(jnp.logical_and(has_down, zz >= z))(lambda: copy(i, p, 1).wait_send())
            if Y > 1:
                copy(i, p, 2).wait_send()
        if C > 1:
            for u in range(units):
                copy(u * C + c, p, 3).wait_send()


def shards(dims, orbitals, basis, kernel_block):
    Z, Y, C = dims
    n = Z * Y * C
    rows, nocc = orbitals.shape
    nb = basis.shape[1]
    points = kernel_block.shape[1]
    half = nb // 2
    cw = nb // n
    bf16 = jnp.bfloat16
    any_space = pl.BlockSpec(memory_space=pl.ANY)
    return pl.pallas_call(
        functools.partial(kernel, dims),
        out_shape=jax.ShapeDtypeStruct((nb, cw), jnp.float32),
        in_specs=[any_space] * 3,
        out_specs=pl.BlockSpec(memory_space=pltpu.VMEM),
        scratch_shapes=[
            pltpu.VMEM((n, rows, nocc), bf16),
            pltpu.VMEM((2, n, rows, half), bf16),
            pltpu.VMEM((rows, points), bf16),
            pltpu.VMEM((rows, points), bf16),
            pltpu.VMEM((2, half, rows), bf16),
            pltpu.VMEM((cw, points), bf16),
            pltpu.SemaphoreType.DMA((2 + nb // LANES,)),
            pltpu.SemaphoreType.DMA((4, 3, Z * Y)),
            pltpu.SemaphoreType.DMA((3, n)),
            pltpu.SemaphoreType.DMA((2, n // 2)),
            pltpu.SemaphoreType.DMA((n,)),
        ],
        compiler_params=pltpu.CompilerParams(
            collective_id=0, has_side_effects=True, vmem_limit_bytes=60 * 1024 * 1024
        ),
    )(orbitals, basis, kernel_block)


def solution(mesh):
    spec = P(("groups", "row"), None)
    return jax.shard_map(
        functools.partial(shards, layout(mesh)),
        mesh=mesh,
        in_specs=(spec, spec, spec),
        out_specs=P("groups", "row"),
        check_vma=False,
    )
```

```python
import functools

import jax
import jax.numpy as jnp
from jax import lax
from jax.experimental import pallas as pl
from jax.experimental.pallas import tpu as pltpu
from jax.sharding import PartitionSpec as P

LANES = 128
MESH = pl.DeviceIdType.MESH


def layout(mesh):
    n = mesh.shape["row"]
    try:
        line = mesh.devices[0]
        places = [tuple(d.coords) + (d.core_on_chip,) for d in line]
    except AttributeError:
        return n, 1, 1
    cores = len({p[-1] for p in places})
    axes = [a for a in range(3) if len({p[a] for p in places}) > 1]
    sizes = {a: len({p[a] for p in places}) for a in axes}
    for axis_z in axes:
        rest = [a for a in axes if a != axis_z]
        if len(rest) > 1 or (rest and sizes[rest[0]] != 2):
            continue
        y_size = sizes[rest[0]] if rest else 1
        z0 = min(p[axis_z] for p in places)
        y0 = min(p[rest[0]] for p in places) if rest else 0
        found = [
            ((p[axis_z] - z0) * y_size + (p[rest[0]] - y0 if rest else 0)) * cores + p[-1]
            for p in places
        ]
        if found == list(range(n)):
            return sizes[axis_z], y_size, cores
    return n, 1, 1


def kernel(
    dims, o_in, b_in, k_in, out_ref,
    o_all, b_all, k_v, w, app_t, got, in_sem, send_sem, recv_sem, a2a_send, a2a_recv,
):
    Z, Y, C = dims
    n = Z * Y * C
    units = Z * Y
    parts = 3
    rows = o_in.shape[0]
    half_cols = b_all.shape[-1]
    groups = half_cols // LANES
    cw = app_t.shape[0] * app_t.shape[1] // n
    per = LANES // cw

    me = lax.axis_index("row")
    c = me % C
    y = (me // C) % Y
    z = me // (C * Y)
    peer_y = (Y - 1) - y

    def index(zz, yy, cc):
        return (zz * Y + yy) * C + cc

    up_dev = index(jnp.minimum(z + 1, Z - 1), y, c)
    down_dev = index(jnp.maximum(z - 1, 0), y, c)
    y_dev = index(z, peer_y, c)
    sib_dev = index(z, y, (C - 1) - c)
    has_up = z < Z - 1
    has_down = z > 0

    def chunk(i, p):
        return o_all.at[i] if p == 0 else b_all.at[p - 1, i]

    def copy(i, p, kind):
        dev = (up_dev, down_dev, y_dev, sib_dev)[kind]
        return pltpu.make_async_remote_copy(
            src_ref=chunk(i, p),
            dst_ref=chunk(i, p),
            send_sem=send_sem.at[kind, p, i // C],
            recv_sem=recv_sem.at[p, i],
            device_id={"row": dev},
            device_id_type=MESH,
        )

    def wait_recv(i, p):
        copy(i, p, 3).wait_recv()

    loads = [pltpu.make_async_copy(o_in, o_all.at[me], in_sem.at[0])]
    for g in range(2 * groups):
        h, s = g % 2, g // 2
        loads.append(
            pltpu.make_async_copy(
                b_in.at[:, pl.ds(g * LANES, LANES)],
                b_all.at[h, me, :, pl.ds(s * LANES, LANES)],
                in_sem.at[1 + g],
            )
        )
    k_load = pltpu.make_async_copy(k_in, k_v, in_sem.at[1 + 2 * groups])
    for load in loads:
        load.start()
    k_load.start()

    barrier = pltpu.get_barrier_semaphore()

    def greet(dev):
        pl.semaphore_signal(barrier, inc=1, device_id={"row": dev}, device_id_type=MESH)

    pl.when(has_up)(lambda: greet(up_dev))
    pl.when(has_down)(lambda: greet(down_dev))
    if Y > 1:
        greet(y_dev)
    if C > 1:
        greet(sib_dev)
    others = (Y > 1) + (C > 1)
    pl.semaphore_wait(barrier, others + has_up.astype(jnp.int32) + has_down.astype(jnp.int32))

    relays = Y > 1 and Z >= 4
    both, either = jnp.logical_and, jnp.logical_or

    def goes_across(zz, p):
        if not relays:
            return True
        turn = c == p % C
        end = either(both(both(z == 0, zz == 1), turn), both(both(z == Z - 1, zz == Z - 2), turn))
        beside = either(both(z == 1, zz == 0), both(z == Z - 2, zz == Z - 1))
        return jnp.logical_not(either(end, beside))

    def relay_up(p):
        return either(z == 0, both(z == Z - 2, c == p % C))

    def relay_down(p):
        return either(z == Z - 1, both(z == 1, c == p % C))

    def spread(i, zz, p, up=False, down=False, across=False):
        if up:
            pl.when(has_up)(lambda: copy(i, p, 0).start())
        if down:
            pl.when(has_down)(lambda: copy(i, p, 1).start())
        if across and Y > 1:
            pl.when(goes_across(zz, p))(lambda: copy(i, p, 2).start())
        if C > 1:
            copy(i, p, 3).start()

    def own(p):
        if p == 0:
            loads[0].wait()
        else:
            for g in range(2 * groups):
                if g % 2 == p - 1:
                    loads[1 + g].wait()
        spread(me, z, p, up=True, down=True, across=True)

    def along(p, t):
        def low():
            i = index(z - t, y, c)
            wait_recv(i, p)
            spread(i, z - t, p, up=True, across=True)

        def high():
            i = index(z + t, y, c)
            wait_recv(i, p)
            spread(i, z + t, p, down=True, across=True)

        pl.when(z - t >= 0)(low)
        pl.when(z + t < Z)(high)

    def across(p, t):
        def one(zz):
            i = index(zz, peer_y, c)
            wait_recv(i, p)
            if relays and t == 0:
                pl.when(relay_up(p))(lambda: copy(i, p, 0).start())
                pl.when(relay_down(p))(lambda: copy(i, p, 1).start())
            spread(i, zz, p)

        if t == 0:
            one(z)
        else:
            pl.when(z - t >= 0)(lambda: one(z - t))
            pl.when(z + t < Z)(lambda: one(z + t))

    events = []
    for p in range(parts):
        base = p * ((Z - 0.5) if relays else (Z if Y > 1 else max(Z - 1, 1)))
        events.append((base - 0.7 * (p > 0), p, functools.partial(own, p)))
        for t in range(1, Z):
            events.append((base + t, p, functools.partial(along, p, t)))
        if Y > 1:
            for t in range(Z):
                events.append((base + t + 1 + 0.6 * (t > 0), p, functools.partial(across, p, t)))
    events.sort(key=lambda e: e[0])
    last = [max(k for k, e in enumerate(events) if e[1] == p) for p in range(parts)]

    def wait_sibling(p, u):
        if C > 1:
            wait_recv(u * C + (C - 1) - c, p)

    def weigh(u):
        if u == 0:
            k_load.wait()
        wait_sibling(0, u)
        cols = pl.ds(u * C * rows, C * rows)
        block = o_all[u * C:(u + 1) * C].reshape(C * rows, o_all.shape[-1])
        density = lax.dot_general(
            o_all[me], block, (((1,), (1,)), ((), ())), preferred_element_type=jnp.float32
        )
        w[:, cols] = (density * k_v[:, cols].astype(jnp.float32)).astype(jnp.bfloat16)

    wide = 2 * LANES if groups % 2 == 0 else LANES
    depth = min(n, max(1, 2048 // rows))

    def apply(h, j):
        if j == 0:
            for u in range(units):
                wait_sibling(1 + h, u)
        cols = pl.ds(j * wide, wide)

        def term(q):
            block = b_all[h, pl.ds(q * depth, depth), :, cols].reshape(depth * rows, wide)
            return jnp.dot(
                w[:, pl.ds(pl.multiple_of(q * depth * rows, LANES), depth * rows)],
                block,
                preferred_element_type=jnp.float32,
            )

        if n == depth:
            total = term(0)
        else:
            total = lax.fori_loop(
                0, n // depth, lambda q, a: a + term(q), jnp.zeros((rows, wide), jnp.float32)
            )
        app_t[h, cols, :] = total.astype(jnp.bfloat16).T

    count = n // 2

    def exchange(h, q):
        qq = (q + me) % count
        s, e = qq // per, qq % per
        d = (2 * s + h) * per + e
        off = pl.multiple_of(s * LANES + e * cw, 16)
        return d, pltpu.make_async_remote_copy(
            src_ref=app_t.at[h, pl.ds(off, cw), :],
            dst_ref=got.at[:, pl.ds(pl.multiple_of(me * rows, LANES), rows)],
            send_sem=a2a_send.at[h, q],
            recv_sem=a2a_recv.at[me],
            device_id={"row": d},
            device_id_type=MESH,
        ), pltpu.make_async_copy(
            app_t.at[h, pl.ds(off, cw), :],
            got.at[:, pl.ds(pl.multiple_of(me * rows, LANES), rows)],
            a2a_recv.at[me],
        )

    def hand_out(h):
        for q in range(count):
            d, remote, local = exchange(h, q)
            pl.when(d != me)(lambda: remote.start())
            pl.when(d == me)(lambda: local.start())

    work = {p: [] for p in range(parts)}
    for u in range(units):
        work[0].append(functools.partial(weigh, u))
    for h in range(2):
        for j in range(half_cols // wide):
            work[1 + h].append(functools.partial(apply, h, j))
        work[1 + h].append(functools.partial(hand_out, h))

    queue = []
    for k, (_, _, event) in enumerate(events):
        event()
        if queue:
            queue.pop(0)()
        for p in range(parts):
            if last[p] == k:
                queue.extend(work[p])
    for item in queue:
        item()

    for src in range(n):
        pltpu.make_async_copy(
            got.at[:, pl.ds(src * rows, rows)], got.at[:, pl.ds(src * rows, rows)], a2a_recv.at[src]
        ).wait()
    for h in range(2):
        for j in range(half_cols // wide):
            cols = pl.ds(j * wide, wide)

            def term(q):
                block = b_all[h, pl.ds(q * depth, depth), :, cols].reshape(depth * rows, wide)
                return jnp.dot(
                    got[:, pl.ds(pl.multiple_of(q * depth * rows, LANES), depth * rows)],
                    block,
                    preferred_element_type=jnp.float32,
                )

            if n == depth:
                total = term(0)
            else:
                total = lax.fori_loop(
                    0, n // depth, lambda q, a: a + term(q), jnp.zeros((cw, wide), jnp.float32)
                )
            for v in range(wide // LANES):
                g = 2 * (j * (wide // LANES) + v) + h
                out_ref[pl.ds(g * LANES, LANES), :] = total[:, v * LANES:(v + 1) * LANES].T

    for h in range(2):
        for q in range(count):
            d, remote, _ = exchange(h, q)
            pl.when(d != me)(lambda: remote.wait_send())
    for p in range(parts):
        for zz in range(Z):
            i = index(zz, y, c)
            pl.when(jnp.logical_and(has_up, zz <= z))(lambda: copy(i, p, 0).wait_send())
            pl.when(jnp.logical_and(has_down, zz >= z))(lambda: copy(i, p, 1).wait_send())
            if Y > 1:
                pl.when(goes_across(zz, p))(lambda: copy(i, p, 2).wait_send())
        if relays:
            i = index(z, peer_y, c)
            pl.when(relay_up(p))(lambda: copy(i, p, 0).wait_send())
            pl.when(relay_down(p))(lambda: copy(i, p, 1).wait_send())
        if C > 1:
            for u in range(units):
                copy(u * C + c, p, 3).wait_send()


def shards(dims, orbitals, basis, kernel_block):
    Z, Y, C = dims
    n = Z * Y * C
    rows, nocc = orbitals.shape
    nb = basis.shape[1]
    points = kernel_block.shape[1]
    half = nb // 2
    cw = nb // n
    bf16 = jnp.bfloat16
    any_space = pl.BlockSpec(memory_space=pl.ANY)
    return pl.pallas_call(
        functools.partial(kernel, dims),
        out_shape=jax.ShapeDtypeStruct((nb, cw), jnp.float32),
        in_specs=[any_space] * 3,
        out_specs=pl.BlockSpec(memory_space=pltpu.VMEM),
        scratch_shapes=[
            pltpu.VMEM((n, rows, nocc), bf16),
            pltpu.VMEM((2, n, rows, half), bf16),
            pltpu.VMEM((rows, points), bf16),
            pltpu.VMEM((rows, points), bf16),
            pltpu.VMEM((2, half, rows), bf16),
            pltpu.VMEM((cw, points), bf16),
            pltpu.SemaphoreType.DMA((2 + nb // LANES,)),
            pltpu.SemaphoreType.DMA((4, 3, Z * Y)),
            pltpu.SemaphoreType.DMA((3, n)),
            pltpu.SemaphoreType.DMA((2, n // 2)),
            pltpu.SemaphoreType.DMA((n,)),
        ],
        compiler_params=pltpu.CompilerParams(
            collective_id=0, has_side_effects=True, vmem_limit_bytes=60 * 1024 * 1024
        ),
    )(orbitals, basis, kernel_block)


def solution(mesh):
    spec = P(("groups", "row"), None)
    return jax.shard_map(
        functools.partial(shards, layout(mesh)),
        mesh=mesh,
        in_specs=(spec, spec, spec),
        out_specs=P("groups", "row"),
        check_vma=False,
    )
```

```python
import functools

import jax
import jax.numpy as jnp
from jax import lax
from jax.experimental import pallas as pl
from jax.experimental.pallas import tpu as pltpu
from jax.sharding import PartitionSpec as P

LANES = 128
LEAD, LEAD_Y, LATE, ACROSS = (0, 7, 7), (0, 7, 7), 0, (2.1, 5.6)
MESH = pl.DeviceIdType.MESH


def layout(mesh):
    n = mesh.shape["row"]
    try:
        line = mesh.devices[0]
        places = [tuple(d.coords) + (d.core_on_chip,) for d in line]
    except AttributeError:
        return n, 1, 1
    cores = len({p[-1] for p in places})
    axes = [a for a in range(3) if len({p[a] for p in places}) > 1]
    sizes = {a: len({p[a] for p in places}) for a in axes}
    for axis_z in axes:
        rest = [a for a in axes if a != axis_z]
        if len(rest) > 1 or (rest and sizes[rest[0]] != 2):
            continue
        y_size = sizes[rest[0]] if rest else 1
        z0 = min(p[axis_z] for p in places)
        y0 = min(p[rest[0]] for p in places) if rest else 0
        found = [
            ((p[axis_z] - z0) * y_size + (p[rest[0]] - y0 if rest else 0)) * cores + p[-1]
            for p in places
        ]
        if found == list(range(n)):
            return sizes[axis_z], y_size, cores
    return n, 1, 1


def kernel(
    dims, o_in, b_in, k_in, out_ref,
    o_all, b_all, k_v, w, app_t, got, in_sem, send_sem, recv_sem, a2a_send, a2a_recv,
):
    Z, Y, C = dims
    n = Z * Y * C
    units = Z * Y
    parts = 3
    rows = o_in.shape[0]
    half_cols = b_all.shape[-1]
    groups = half_cols // LANES
    cw = app_t.shape[0] * app_t.shape[1] // n
    per = LANES // cw

    me = lax.axis_index("row")
    c = me % C
    y = (me // C) % Y
    z = me // (C * Y)
    peer_y = (Y - 1) - y

    def index(zz, yy, cc):
        return (zz * Y + yy) * C + cc

    up_dev = index(jnp.minimum(z + 1, Z - 1), y, c)
    down_dev = index(jnp.maximum(z - 1, 0), y, c)
    y_dev = index(z, peer_y, c)
    sib_dev = index(z, y, (C - 1) - c)
    has_up = z < Z - 1
    has_down = z > 0

    def chunk(i, p):
        return o_all.at[i] if p == 0 else b_all.at[p - 1, i]

    def copy(i, p, kind):
        dev = (up_dev, down_dev, y_dev, sib_dev)[kind]
        return pltpu.make_async_remote_copy(
            src_ref=chunk(i, p),
            dst_ref=chunk(i, p),
            send_sem=send_sem.at[kind, p, i // C],
            recv_sem=recv_sem.at[p, i],
            device_id={"row": dev},
            device_id_type=MESH,
        )

    def wait_recv(i, p):
        copy(i, p, 3).wait_recv()

    loads = [pltpu.make_async_copy(o_in, o_all.at[me], in_sem.at[0])]
    for g in range(2 * groups):
        h, s = g % 2, g // 2
        loads.append(
            pltpu.make_async_copy(
                b_in.at[:, pl.ds(g * LANES, LANES)],
                b_all.at[h, me, :, pl.ds(s * LANES, LANES)],
                in_sem.at[1 + g],
            )
        )
    k_load = pltpu.make_async_copy(k_in, k_v, in_sem.at[1 + 2 * groups])
    for load in loads:
        load.start()
    k_load.start()

    barrier = pltpu.get_barrier_semaphore()

    def greet(dev):
        pl.semaphore_signal(barrier, inc=1, device_id={"row": dev}, device_id_type=MESH)

    pl.when(has_up)(lambda: greet(up_dev))
    pl.when(has_down)(lambda: greet(down_dev))
    if Y > 1:
        greet(y_dev)
    if C > 1:
        greet(sib_dev)
    others = (Y > 1) + (C > 1)
    pl.semaphore_wait(barrier, others + has_up.astype(jnp.int32) + has_down.astype(jnp.int32))

    relays = Y > 1 and Z >= 4
    both, either = jnp.logical_and, jnp.logical_or

    def goes_across(zz, p):
        if not relays:
            return True
        turn = c == p % C
        end = either(both(both(z == 0, zz == 1), turn), both(both(z == Z - 1, zz == Z - 2), turn))
        beside = either(both(z == 1, zz == 0), both(z == Z - 2, zz == Z - 1))
        return jnp.logical_not(either(end, beside))

    def relay_up(p):
        return either(z == 0, both(z == Z - 2, c == p % C))

    def relay_down(p):
        return either(z == Z - 1, both(z == 1, c == p % C))

    def spread(i, zz, p, up=False, down=False, across=False):
        if up:
            pl.when(has_up)(lambda: copy(i, p, 0).start())
        if down:
            pl.when(has_down)(lambda: copy(i, p, 1).start())
        if across and Y > 1:
            pl.when(goes_across(zz, p))(lambda: copy(i, p, 2).start())
        if C > 1:
            copy(i, p, 3).start()

    def own(p):
        if p == 0:
            loads[0].wait()
        else:
            for g in range(2 * groups):
                if g % 2 == p - 1:
                    loads[1 + g].wait()
        pl.when(has_up)(lambda: copy(me, p, 0).start())
        pl.when(has_down)(lambda: copy(me, p, 1).start())
        if C > 1:
            copy(me, p, 3).start()

    def own_across(p):
        copy(me, p, 2).start()

    def along(p, t):
        def low():
            i = index(z - t, y, c)
            wait_recv(i, p)
            spread(i, z - t, p, up=True, across=True)

        def high():
            i = index(z + t, y, c)
            wait_recv(i, p)
            spread(i, z + t, p, down=True, across=True)

        pl.when(z - t >= 0)(low)
        pl.when(z + t < Z)(high)

    def across(p, t):
        def one(zz):
            i = index(zz, peer_y, c)
            wait_recv(i, p)
            if relays and t == 0:
                pl.when(relay_up(p))(lambda: copy(i, p, 0).start())
                pl.when(relay_down(p))(lambda: copy(i, p, 1).start())
            spread(i, zz, p)

        if t == 0:
            one(z)
        else:
            pl.when(z - t >= 0)(lambda: one(z - t))
            pl.when(z + t < Z)(lambda: one(z + t))

    stride = (Z - 0.5) if relays else (Z if Y > 1 else max(Z - 1, 1))
    events = []
    for p in range(parts):
        base = p * stride
        events.append((base - LEAD[p], p, functools.partial(own, p)))
        for t in range(1, Z):
            events.append((base + t + LATE * (t > 1), p, functools.partial(along, p, t)))
        if Y > 1:
            events.append((base - LEAD_Y[p] + 0.01, p, functools.partial(own_across, p)))
            for t in range(Z):
                events.append((base + t + ACROSS[t > 0], p, functools.partial(across, p, t)))
    events.sort(key=lambda e: e[0])
    last = [max(k for k, e in enumerate(events) if e[1] == p) for p in range(parts)]

    def wait_sibling(p, u):
        if C > 1:
            wait_recv(u * C + (C - 1) - c, p)

    def weigh(u):
        if u == 0:
            k_load.wait()
        wait_sibling(0, u)
        cols = pl.ds(u * C * rows, C * rows)
        block = o_all[u * C:(u + 1) * C].reshape(C * rows, o_all.shape[-1])
        density = lax.dot_general(
            o_all[me], block, (((1,), (1,)), ((), ())), preferred_element_type=jnp.float32
        )
        w[:, cols] = (density * k_v[:, cols].astype(jnp.float32)).astype(jnp.bfloat16)

    wide = 2 * LANES if groups % 2 == 0 else LANES
    depth = min(n, max(1, 2048 // rows))

    def apply(h, j):
        if j == 0:
            for u in range(units):
                wait_sibling(1 + h, u)
        cols = pl.ds(j * wide, wide)

        def term(q):
            block = b_all[h, pl.ds(q * depth, depth), :, cols].reshape(depth * rows, wide)
            return jnp.dot(
                w[:, pl.ds(pl.multiple_of(q * depth * rows, LANES), depth * rows)],
                block,
                preferred_element_type=jnp.float32,
            )

        if n == depth:
            total = term(0)
        else:
            total = lax.fori_loop(
                0, n // depth, lambda q, a: a + term(q), jnp.zeros((rows, wide), jnp.float32)
            )
        app_t[h, cols, :] = total.astype(jnp.bfloat16).T

    count = n // 2

    def exchange(h, q):
        qq = (q + me) % count
        s, e = qq // per, qq % per
        d = (2 * s + h) * per + e
        off = pl.multiple_of(s * LANES + e * cw, 16)
        return d, pltpu.make_async_remote_copy(
            src_ref=app_t.at[h, pl.ds(off, cw), :],
            dst_ref=got.at[:, pl.ds(pl.multiple_of(me * rows, LANES), rows)],
            send_sem=a2a_send.at[h, q],
            recv_sem=a2a_recv.at[me],
            device_id={"row": d},
            device_id_type=MESH,
        ), pltpu.make_async_copy(
            app_t.at[h, pl.ds(off, cw), :],
            got.at[:, pl.ds(pl.multiple_of(me * rows, LANES), rows)],
            a2a_recv.at[me],
        )

    def hand_out(h):
        for q in range(count):
            d, remote, local = exchange(h, q)
            pl.when(d != me)(lambda: remote.start())
            pl.when(d == me)(lambda: local.start())

    work = {p: [] for p in range(parts)}
    for u in range(units):
        work[0].append(functools.partial(weigh, u))
    for h in range(2):
        for j in range(half_cols // wide):
            work[1 + h].append(functools.partial(apply, h, j))
        work[1 + h].append(functools.partial(hand_out, h))

    queue = []
    for k, (_, _, event) in enumerate(events):
        event()
        if queue:
            queue.pop(0)()
        for p in range(parts):
            if last[p] == k:
                queue.extend(work[p])
    for item in queue:
        item()

    for src in range(n):
        pltpu.make_async_copy(
            got.at[:, pl.ds(src * rows, rows)], got.at[:, pl.ds(src * rows, rows)], a2a_recv.at[src]
        ).wait()
    for h in range(2):
        for j in range(half_cols // wide):
            cols = pl.ds(j * wide, wide)

            def term(q):
                block = b_all[h, pl.ds(q * depth, depth), :, cols].reshape(depth * rows, wide)
                return jnp.dot(
                    got[:, pl.ds(pl.multiple_of(q * depth * rows, LANES), depth * rows)],
                    block,
                    preferred_element_type=jnp.float32,
                )

            if n == depth:
                total = term(0)
            else:
                total = lax.fori_loop(
                    0, n // depth, lambda q, a: a + term(q), jnp.zeros((cw, wide), jnp.float32)
                )
            for v in range(wide // LANES):
                g = 2 * (j * (wide // LANES) + v) + h
                out_ref[:, pl.ds(g * LANES, LANES)] = total[:, v * LANES:(v + 1) * LANES]

    for h in range(2):
        for q in range(count):
            d, remote, _ = exchange(h, q)
            pl.when(d != me)(lambda: remote.wait_send())
    for p in range(parts):
        for zz in range(Z):
            i = index(zz, y, c)
            pl.when(jnp.logical_and(has_up, zz <= z))(lambda: copy(i, p, 0).wait_send())
            pl.when(jnp.logical_and(has_down, zz >= z))(lambda: copy(i, p, 1).wait_send())
            if Y > 1:
                pl.when(goes_across(zz, p))(lambda: copy(i, p, 2).wait_send())
        if relays:
            i = index(z, peer_y, c)
            pl.when(relay_up(p))(lambda: copy(i, p, 0).wait_send())
            pl.when(relay_down(p))(lambda: copy(i, p, 1).wait_send())
        if C > 1:
            for u in range(units):
                copy(u * C + c, p, 3).wait_send()


def shards(dims, orbitals, basis, kernel_block):
    Z, Y, C = dims
    n = Z * Y * C
    rows, nocc = orbitals.shape
    nb = basis.shape[1]
    points = kernel_block.shape[1]
    half = nb // 2
    cw = nb // n
    bf16 = jnp.bfloat16
    any_space = pl.BlockSpec(memory_space=pl.ANY)
    return pl.pallas_call(
        functools.partial(kernel, dims),
        out_shape=jax.ShapeDtypeStruct((cw, nb), jnp.float32),
        in_specs=[any_space] * 3,
        out_specs=pl.BlockSpec(memory_space=pltpu.VMEM),
        scratch_shapes=[
            pltpu.VMEM((n, rows, nocc), bf16),
            pltpu.VMEM((2, n, rows, half), bf16),
            pltpu.VMEM((rows, points), bf16),
            pltpu.VMEM((rows, points), bf16),
            pltpu.VMEM((2, half, rows), bf16),
            pltpu.VMEM((cw, points), bf16),
            pltpu.SemaphoreType.DMA((2 + nb // LANES,)),
            pltpu.SemaphoreType.DMA((4, 3, Z * Y)),
            pltpu.SemaphoreType.DMA((3, n)),
            pltpu.SemaphoreType.DMA((2, n // 2)),
            pltpu.SemaphoreType.DMA((n,)),
        ],
        compiler_params=pltpu.CompilerParams(
            collective_id=0, has_side_effects=True, vmem_limit_bytes=60 * 1024 * 1024
        ),
    )(orbitals, basis, kernel_block).T


def solution(mesh):
    spec = P(("groups", "row"), None)
    return jax.shard_map(
        functools.partial(shards, layout(mesh)),
        mesh=mesh,
        in_specs=(spec, spec, spec),
        out_specs=P("groups", "row"),
        check_vma=False,
    )
```
